32 devices in a mesh: ex: 4 (over z), ey: 2 (over y), ez: 4 (over x, core).
Axes of the slice: x: 2, y: 2, z: 4, core: 2. Of those that a mesh axis runs over, the one named last changes fastest.
Arguments:
- residual: float32 [64, 32, 512], P('ez', 'ey', 'ex'), may hold values from -6 to 6
- local_stream: float32 [18, 18], replicated, may hold values from -1.5 to 1.5
- local_normal: float32 [2, 18, 18], P('ey'), may hold values from -1.5 to 1.5
- local_span: float32 [18, 18], replicated, may hold values from -1.5 to 1.5
- eigen_stream: float32 [18], replicated, may hold values from 0.3 to 3
- eigen_normal: float32 [2, 18], P('ey'), may hold values from 0.3 to 3
- eigen_span: float32 [18], replicated, may hold values from 0.3 to 3
- vertex_stream: float32 [32, 32], replicated, may hold values from -1 to 1
- vertex_normal: float32 [2, 2], replicated, may hold values from -4 to 4
- vertex_span: float32 [4, 4], replicated, may hold values from -3 to 3
- level_stream: float32 [32], replicated, may hold values from 4 to 40
- level_normal: float32 [2], replicated, may hold values from 4 to 40
- level_span: float32 [4], replicated, may hold values from 4 to 40
Outputs:
- applied: float32 [64, 32, 512], P('ez', 'ey', 'ex')
The draws below stay inside these ranges and needn't reach their ends.
All inputs are finite; a program needn't handle non-finite values.
Results may differ from the reference program's by a relative error of at most 0.0003.
Values sent between devices are 32-bit elements; how exact they have to be, the bound alone decides.
A program may use at most 64 MiB of HBM per device.

```python
import math
import jax
import jax.numpy as jnp
from jax import lax

NODES = 16
BLOCK = 18
EX_TOT = 32
EY_TOT = 2
EZ_TOT = 4
XP = 512
YP = 32
ZP = 64


def block_scale(stream_key, extent, cuts, smallest, top_value):
    def one(position, blocks):
        draws = jax.random.uniform(jax.random.fold_in(jax.random.fold_in(stream_key, 6), position), (blocks,), jnp.float32, smallest / len(cuts), top_value / len(cuts))
        return jnp.repeat(jnp.exp(draws), extent[position] // blocks).reshape((-1,) + (1,) * (len(extent) - position - 1))

    level = one(*cuts[0])
    for cut in cuts[1:]:
        level = level * one(*cut)
    return level


def centred(stream_key, dims, scale, reach, shards=(), held_as=jnp.bfloat16):
    array = scale * jax.random.normal(stream_key, dims, jnp.float32)
    if shards:
        array = array * block_scale(stream_key, dims, shards, -0.22, 0.18)
    return jnp.clip(array, -reach, reach).astype(held_as)


def setup_inputs(seed: int = 0) -> dict:
    arg_keys = jax.random.split(jax.random.key(seed), 14)
    return {
        "residual": centred(arg_keys[0], (ZP, YP, XP), 1.0, 6.0, ((0, 4), (1, 2), (2, 4)), jnp.float32),
        "local_stream": centred(arg_keys[1], (BLOCK, BLOCK), BLOCK ** -0.5, 1.5, (), jnp.float32),
        "local_normal": centred(arg_keys[2], (EY_TOT, BLOCK, BLOCK), BLOCK ** -0.5, 1.5, ((0, 2),), jnp.float32),
        "local_span": centred(arg_keys[3], (BLOCK, BLOCK), BLOCK ** -0.5, 1.5, (), jnp.float32),
        "eigen_stream": jnp.clip(jnp.exp(jax.random.uniform(arg_keys[4], (BLOCK,), jnp.float32, math.log(0.3), math.log(3.0))), 0.3, 3.0),
        "eigen_normal": jnp.clip(jnp.exp(math.log(3.0) - 2.3025851 * jax.random.uniform(arg_keys[5], (EY_TOT, BLOCK), jnp.float32) ** block_scale(arg_keys[5], (EY_TOT, BLOCK), ((0, 2),), -0.2, 0.2)), 0.3, 3.0),
        "eigen_span": jnp.clip(jnp.exp(jax.random.uniform(arg_keys[6], (BLOCK,), jnp.float32, math.log(0.3), math.log(3.0))), 0.3, 3.0),
        "vertex_stream": centred(arg_keys[7], (EX_TOT, EX_TOT), EX_TOT ** -0.5, 1.0, (), jnp.float32),
        "vertex_normal": centred(arg_keys[8], (EY_TOT, EY_TOT), EY_TOT ** -0.5, 4.0, (), jnp.float32),
        "vertex_span": centred(arg_keys[9], (EZ_TOT, EZ_TOT), EZ_TOT ** -0.5, 3.0, (), jnp.float32),
        "level_stream": jnp.clip(jnp.exp(jax.random.uniform(arg_keys[10], (EX_TOT,), jnp.float32, math.log(4.0), math.log(40.0))), 4.0, 40.0),
        "level_normal": jnp.clip(jnp.exp(jax.random.uniform(arg_keys[11], (EY_TOT,), jnp.float32, math.log(4.0), math.log(40.0))), 4.0, 40.0),
        "level_span": jnp.clip(jnp.exp(jax.random.uniform(arg_keys[12], (EZ_TOT,), jnp.float32, math.log(4.0), math.log(40.0))), 4.0, 40.0),
    }


HIGHEST = lax.Precision.HIGHEST


def corner_weights(points):
    nodes_at = -jnp.cos(jnp.pi * jnp.arange(points, dtype=jnp.float32) / (points - 1))
    return jnp.stack([(1.0 - nodes_at) / 2.0, (1.0 + nodes_at) / 2.0], axis=1)


def split_windows(values, number):
    points = (values.shape[-1] - 2) // number
    inside = values[..., 1:-1].reshape(values.shape[:-1] + (number, points))
    lower_rim = values[..., 0:points * number:points][..., None]
    upper_rim = values[..., points + 1::points][..., None]
    return jnp.concatenate([lower_rim, inside, upper_rim], axis=-1)


def merge_windows(blocks, number):
    points = blocks.shape[-1] - 2
    inside = blocks[..., 1:-1].reshape(blocks.shape[:-2] + (number * points,))
    padded = jnp.pad(inside, [(0, 0)] * (inside.ndim - 1) + [(1, 1)])
    padded = padded.at[..., 0:points * number:points].add(blocks[..., 0])
    padded = padded.at[..., points + 1::points].add(blocks[..., -1])
    return padded


def local_solve(blocks, stream, normal, span, eig_stream, eig_normal, eig_span):
    modal = jnp.einsum('aibjck,ip->apbjck', blocks, stream, precision=HIGHEST)
    modal = jnp.einsum('apbjck,bjq->apbqck', modal, normal, precision=HIGHEST)
    modal = jnp.einsum('apbqck,kr->apbqcr', modal, span, precision=HIGHEST)
    divisor = (eig_stream[None, :, None, None, None, None] + eig_normal[None, None, :, :, None, None]
               + eig_span[None, None, None, None, None, :])
    modal = modal / divisor
    modal = jnp.einsum('apbqcr,kr->apbqck', modal, span, precision=HIGHEST)
    modal = jnp.einsum('apbqck,bjq->apbjck', modal, normal, precision=HIGHEST)
    return jnp.einsum('apbjck,ip->aibjck', modal, stream, precision=HIGHEST)


def restrict(shaped, weights):
    partial_sum = jnp.einsum('zkyjxi,ia->zkyjxa', shaped, weights, precision=HIGHEST)
    partial_sum = jnp.einsum('zkyjxa,jb->zkybxa', partial_sum, weights, precision=HIGHEST)
    return jnp.einsum('zkybxa,kc->zcybxa', partial_sum, weights, precision=HIGHEST)


def prolong(corner_vals, weights):
    partial_sum = jnp.einsum('zcybxa,ia->zcybxi', corner_vals, weights, precision=HIGHEST)
    partial_sum = jnp.einsum('zcybxi,jb->zcyjxi', partial_sum, weights, precision=HIGHEST)
    return jnp.einsum('zcyjxi,kc->zkyjxi', partial_sum, weights, precision=HIGHEST)


def fold_periodic(values):
    inside = values[..., 1:-1]
    inside = inside.at[..., 0].add(values[..., -1])
    return inside.at[..., -1].add(values[..., 0])


def reference(residual, local_stream, local_normal, local_span, eigen_stream, eigen_normal, eigen_span,
              vertex_stream, vertex_normal, vertex_span, level_stream, level_normal, level_span):
    points = NODES
    padded = jnp.pad(residual, ((1, 1), (0, 0), (1, 1)), mode="wrap")
    padded = jnp.pad(padded, ((0, 0), (1, 1), (0, 0)))

    def one_layer(layer_index):
        slab_values = lax.dynamic_slice_in_dim(padded, layer_index * points, points + 2, 0)
        blocks = split_windows(slab_values, EX_TOT)
        blocks = jnp.moveaxis(blocks, 1, -1)
        blocks = split_windows(blocks, EY_TOT)
        blocks = jnp.moveaxis(blocks, 0, -1)[..., None, :]
        solved = local_solve(blocks, local_stream, local_normal, local_span,
                             eigen_stream, eigen_normal, eigen_span)[..., 0, :]
        solved = jnp.moveaxis(solved, -1, 0)
        solved = merge_windows(solved, EY_TOT)
        solved = jnp.moveaxis(solved, -1, 1)
        return merge_windows(solved, EX_TOT)

    layers = lax.map(one_layer, jnp.arange(EZ_TOT, dtype=jnp.int32))
    layers = jnp.moveaxis(layers, (0, 1), (-2, -1))
    gathered = jnp.moveaxis(merge_windows(layers, EZ_TOT), -1, 0)
    schwarz = fold_periodic(gathered)
    schwarz = jnp.moveaxis(fold_periodic(jnp.moveaxis(schwarz, 0, -1)), -1, 0)
    schwarz = schwarz[:, 1:-1, :]

    weights = corner_weights(points)
    shaped = residual.reshape(EZ_TOT, points, EY_TOT, points, EX_TOT, points)
    corner = restrict(shaped, weights)
    loads_x = corner[..., 0] + jnp.roll(corner[..., 1], 1, axis=-1)
    lower_part = loads_x[:, :, :, 0, :]
    upper_part = jnp.concatenate([jnp.zeros_like(loads_x[:, :, :1, 1, :]), loads_x[:, :, :-1, 1, :]], axis=2)
    loads_y = lower_part + upper_part
    loads = loads_y[:, 0] + jnp.roll(loads_y[:, 1], 1, axis=0)
    modes = jnp.einsum('zyx,xp->zyp', loads, vertex_stream, precision=HIGHEST)
    modes = jnp.einsum('zyp,yn->znp', modes, vertex_normal, precision=HIGHEST)
    modes = jnp.einsum('znp,zm->mnp', modes, vertex_span, precision=HIGHEST)
    scaled = modes / (level_span[:, None, None] + level_normal[None, :, None] + level_stream[None, None, :])
    coarse = jnp.einsum('mnp,zm->znp', scaled, vertex_span, precision=HIGHEST)
    coarse = jnp.einsum('znp,yn->zyp', coarse, vertex_normal, precision=HIGHEST)
    coarse = jnp.einsum('zyp,xp->zyx', coarse, vertex_stream, precision=HIGHEST)
    extended = jnp.concatenate([coarse, coarse[:1]], axis=0)
    extended = jnp.concatenate([extended, jnp.zeros_like(extended[:, :1])], axis=1)
    extended = jnp.concatenate([extended, extended[:, :, :1]], axis=2)
    pairs_x = jnp.stack([extended[..., :-1], extended[..., 1:]], axis=-1)
    pairs_y = jnp.stack([pairs_x[:, :-1], pairs_x[:, 1:]], axis=2)
    pairs_z = jnp.stack([pairs_y[:-1], pairs_y[1:]], axis=1)
    correction = prolong(pairs_z, weights).reshape(ZP, YP, XP)
    return schwarz + correction
```

```python
import functools
import math

import jax
import jax.numpy as jnp
from jax import lax
from jax.experimental import pallas as pl
from jax.experimental.pallas import tpu as pltpu
from jax.sharding import PartitionSpec as P

F32 = jnp.float32
BF16 = jnp.bfloat16
I32 = jnp.int32
HALO = 24
DIRS = ((1, 0), (-1, 0), (0, 1), (0, -1), (1, 1), (1, -1), (-1, 1), (-1, -1))


def iota(shape, dim):
    return lax.broadcasted_iota(I32, shape, dim)


def quotient(x, d):
    return (x * (65536 // d + 1)) >> 16


def onehot(mask):
    return jnp.where(mask, 1.0, 0.0).astype(F32)


def split(x):
    hi = x.astype(BF16)
    return hi, (x - hi.astype(F32)).astype(BF16)


def dg(a, b, dims):
    return lax.dot_general(a, b, ((dims[:1], dims[1:]), ((), ())), preferred_element_type=F32)


def dot3(a, b, dims=(1, 0)):
    (ah, al), (bh, bl) = a, b
    return dg(ah, bh, dims) + (dg(ah, bl, dims) + dg(al, bh, dims))


def pick(mask, values, dims=(1, 0)):
    hi, lo = split(values)
    mask = mask.astype(BF16)
    return dg(mask, hi, dims) + dg(mask, lo, dims)


def hat(index, points):
    out = jnp.zeros(index.shape, F32)
    for i in range(points):
        out = jnp.where(index == i, (1.0 - math.cos(math.pi * i / (points - 1))) / 2.0, out)
    return out


def kernel(
    sizes,
    res, stream, normal, span, eig_x, eig_y, eig_z,
    v_stream, v_normal, v_span, lev_x, lev_y, lev_z,
    out,
    rim, kh, kl, cx, back, got, parts, mine,
    ssem, rsem,
):
    nx, ny, nz = sizes
    block = stream.shape[0]
    n = block - 2
    sh = n.bit_length() - 1
    length = res.shape[2]
    ne = length // n
    main = n * n
    rows = kh.shape[0]
    nrim = rows - main
    lanes = kh.shape[1]
    edge = main + 4 * n
    nv, nm = v_stream.shape
    mn = nz * ny
    ix, iy, iz = lax.axis_index("ex"), lax.axis_index("ey"), lax.axis_index("ez")

    rim[...] = jnp.zeros_like(rim)
    got[...] = jnp.zeros_like(got)

    def wrap(i, size):
        return lax.rem(i + size, size)

    def has(dy):
        return jnp.logical_and(iy + dy >= 0, iy + dy < ny)

    def guarded(dy, fn):
        if dy == 0:
            fn()
        else:
            pl.when(has(dy))(fn)

    barrier = pltpu.get_barrier_semaphore()

    def signal(where):
        pl.semaphore_signal(
            barrier, inc=1, device_id=where, device_id_type=pl.DeviceIdType.MESH
        )

    for axis, index, size in (("ez", iz, nz), ("ey", iy, ny), ("ex", ix, nx)):
        for d in range(1, size):
            signal({axis: lax.rem(index + d, size)})
    for dz, dy in DIRS[4:]:
        guarded(dy, functools.partial(signal, {"ez": wrap(iz + dz, nz), "ey": iy + dy}))
    inner = jnp.where(iy > 0, 2, 0) + jnp.where(iy < ny - 1, 2, 0)

    data = res[...].reshape(main, length)
    row, col = iota((rows, block), 0), iota((rows, block), 1)
    low = row & (n - 1)
    e0 = row - edge
    rk = jnp.where(row < main, (row >> sh) + 1, low + 1)
    rk = jnp.where((row >= main) & (row < main + n), 0, rk)
    rk = jnp.where((row >= main + n) & (row < main + 2 * n), n + 1, rk)
    rk = jnp.where(row >= edge, jnp.where(e0 < 2, 0, n + 1), rk)
    rk = jnp.where(row >= edge + 4, -1, rk)
    rj = jnp.where((row >= main + 2 * n) & (row < main + 3 * n), 0, low + 1)
    rj = jnp.where((row >= main + 3 * n) & (row < main + 4 * n), n + 1, rj)
    rj = jnp.where(row >= edge, jnp.where((e0 & 1) == 0, 0, n + 1), rj)
    rj = jnp.where(row >= edge + 4, -1, rj)
    sel_k, sel_j = onehot(rk == col), onehot(rj == col)
    brow, bcol = iota((block, lanes), 0), iota((block, lanes), 1)
    bq = quotient(bcol, block)
    to_r = onehot(bq == brow)
    to_q = onehot((bcol - block * bq == brow) & (bcol < block * block))
    span_l = dot3(split(span[...]), split(to_r))
    normal_l = dot3(split(normal[0]), split(to_q))
    kmat = pick(sel_k, span_l) * pick(sel_j, normal_l)
    k_hi, k_lo = split(kmat)
    kh[...] = k_hi
    kl[...] = k_lo

    wn = n
    hrow, hcol = iota((8, main), 0), iota((8, main), 1)
    wk, wj = hat(hcol >> sh, wn), hat(hcol & (n - 1), wn)
    hyz = jnp.where((hrow & 2) > 0, wk, 1.0 - wk) * jnp.where((hrow & 1) > 0, wj, 1.0 - wj)
    hyz = split(jnp.where(hrow < 4, hyz, 0.0))
    xrow, xcol = iota((length, nv), 0), iota((length, nv), 1)
    wx = hat(xrow & (n - 1), wn)
    base = ix * ne + (xrow >> sh)
    after = jnp.where(base + 1 >= nv, base + 1 - nv, base + 1)
    hx = jnp.where(xcol == base, 1.0 - wx, 0.0) + jnp.where(xcol == after, wx, 0.0)
    wxm = split(dot3(split(hx), split(v_stream[...])))
    d_split = split(data)
    loads = dot3(split(dot3(hyz, d_split)), wxm)
    mrow, mcol = iota((mn, nz), 0), iota((mn, nz), 1)
    is_m = onehot((mrow >= mcol * ny) & (mrow < (mcol + 1) * ny))
    nrow, ncol = iota((mn, ny), 0), iota((mn, ny), 1)
    is_n = onehot(nrow - ny * quotient(nrow, ny) == ncol)
    vrow, vcol = iota((nz, 8), 0), iota((nz, 8), 1)
    vz = iz + (vcol >> 1)
    vz = jnp.where(vz >= nz, vz - nz, vz)
    at_z = onehot((vrow == vz) & (vcol < 4))
    urow, ucol = iota((ny, 8), 0), iota((ny, 8), 1)
    at_y = onehot((urow == iy + (ucol & 1)) & (ucol < 4))
    amat = pick(is_m, dot3(split(v_span[...].T), split(at_z)))
    amat = amat * pick(is_n, dot3(split(v_normal[...].T), split(at_y)))
    a_split = split(amat)
    mine[0, :, :nm] = dot3(a_split, split(loads))
    level = jnp.sum(is_m * lev_z[...], axis=1, keepdims=True)
    level = level + jnp.sum(is_n * lev_y[...], axis=1, keepdims=True) + lev_x[...]

    pl.semaphore_wait(barrier, (nx - 1) + (ny - 1) + (nz - 1) + inner)

    def shipped(src, dst, slot, where):
        return pltpu.make_async_remote_copy(
            src_ref=src, dst_ref=dst, send_sem=ssem.at[slot], recv_sem=rsem.at[slot],
            device_id=where, device_id_type=pl.DeviceIdType.MESH,
        )

    def target(dz, dy):
        where = {}
        if dz:
            where["ez"] = wrap(iz + dz, nz)
        if dy:
            where["ey"] = iy + dy
        return where

    def halo(slot):
        dz, dy = DIRS[slot]
        if dy == 0:
            src = res.at[n - 1 if dz > 0 else 0]
            dst = rim.at[pl.ds(0 if dz > 0 else n, n)]
        elif dz == 0:
            src = res.at[:, n - 1 if dy > 0 else 0]
            dst = rim.at[pl.ds(2 * n if dy > 0 else 3 * n, n)]
        else:
            src = res.at[n - 1 if dz > 0 else 0, pl.ds(n - 1 if dy > 0 else 0, 1)]
            dst = rim.at[pl.ds(4 * n + (0 if dz > 0 else 2) + (0 if dy > 0 else 1), 1)]
        return shipped(src, dst, slot, target(dz, dy))

    def ret(slot):
        dz, dy = DIRS[slot]
        if dy == 0:
            at, number = (n if dz > 0 else 0), n
        elif dz == 0:
            at, number = (3 * n if dy > 0 else 2 * n), n
        else:
            at, number = 4 * n + (2 if dz > 0 else 0) + (1 if dy > 0 else 0), 1
        return shipped(
            back.at[pl.ds(at, number)], got.at[pl.ds(at, number)], 8 + slot, target(dz, dy)
        )

    def start_all(make):
        for s, (dz, dy) in enumerate(DIRS):
            guarded(dy, lambda s=s: make(s).start())

    def wait_all(make):
        for s, (dz, dy) in enumerate(DIRS):
            guarded(dy, lambda s=s: make(s).wait_send())
            guarded(-dy, lambda s=s: make(s).wait_recv())

    stages = {"ez": (0, iz, nz), "ex": (1, ix, nx), "ey": (2, iy, ny)}
    offset = {"ez": 0, "ex": nz - 1, "ey": nz + nx - 2}

    def stage_copies(axis):
        st, index, size = stages[axis]
        return [
            shipped(
                mine.at[st], parts.at[offset[axis] + d - 1], 18 + offset[axis] + d - 1,
                {axis: lax.rem(index + d, size)},
            )
            for d in range(1, size)
        ]

    def stage_start(axis):
        for c in stage_copies(axis):
            c.start()

    def stage_end(axis):
        st, index, size = stages[axis]
        total = mine[st, :, :nm]
        for d, c in enumerate(stage_copies(axis)):
            c.wait_recv()
            c.wait_send()
            total = total + parts[offset[axis] + d, :, :nm]
        return total

    start_all(halo)
    stage_start("ez")
    k_main = kh[0:main], kl[0:main]
    k_rim = kh[main:], kl[main:]
    c_main = dot3(split(data.T), k_main)
    nep = cx.shape[0]
    pairs = (ne + 2) * block
    npad = -(-pairs // 16) * 16
    wrow, wcol = iota((npad, nep), 0), iota((npad, nep), 1)
    xs = jnp.where(wcol < length, wcol, jnp.where(wcol < length + HALO, wcol - length - HALO, wcol - HALO))
    xi = xs + 1 + n - n * quotient(wrow, block)
    trow, tcol = iota((block, nep), 0), iota((block, nep), 1)
    tx = jnp.where(tcol < length, tcol, jnp.where(tcol < length + HALO, tcol - length - HALO, tcol - HALO))
    tm = (tx + 1) & (n - 1)
    s_t = split(stream[...].T)
    first = dot3(s_t, split(onehot(trow == tm)))
    second = dot3(s_t, split(onehot(trow - n == tm)))
    prow, pcol = iota((npad, block), 0), iota((npad, block), 1)
    is_p = onehot((prow - block * quotient(prow, block) == pcol) & (prow < pairs))
    wmat = jnp.where((xi >= 0) & (xi < n), pick(is_p, first), 0.0)
    wmat = wmat + jnp.where((xi >= n) & (xi < block), pick(is_p, second), 0.0)
    w_main = split(wmat[:, :length])
    w_halo = split(wmat[:, length:])
    w_back = split(wmat[:, :length].T)
    eig_yz = dot3(split(jnp.broadcast_to(eig_z[...], (8, block))), split(to_r))
    eig_yz = eig_yz + dot3(split(jnp.broadcast_to(eig_y[...], (8, block))), split(to_q))
    ecol = jnp.sum(is_p * eig_x[...], axis=1, keepdims=True)
    ecol = jnp.where(iota((npad, 1), 0) < pairs, ecol, 1.0)
    inverse = 1.0 / (ecol + eig_yz[0:1])

    wait_all(halo)
    cx[0:length] = c_main + dot3(split(rim[...].T), k_rim)

    def x_copies():
        right = {"ex": wrap(ix + 1, nx)}
        left = {"ex": wrap(ix - 1, nx)}
        return (
            shipped(cx.at[pl.ds(length - HALO, HALO)], cx.at[pl.ds(length, HALO)], 16, right),
            shipped(cx.at[pl.ds(0, HALO)], cx.at[pl.ds(length + HALO, HALO)], 17, left),
        )

    for c in x_copies():
        c.start()
    mine[1, :, :nm] = stage_end("ez")
    stage_start("ex")
    modal = dot3(w_main, split(cx[0:length]))
    for c in x_copies():
        c.wait()
    modal = modal + dot3(w_halo, split(cx[length:]))
    u = split(dot3(w_back, split(modal * inverse)))
    back[...] = dot3(k_rim, u, (1, 1))
    start_all(ret)
    mine[2, :, :nm] = stage_end("ex")
    stage_start("ey")
    result = dot3(k_main, u, (1, 1))
    scaled = split(stage_end("ey") / level)
    coarse = dot3(split(amat.T), scaled)
    coarse = dot3(split(coarse), wxm, (1, 1))
    result = result + dot3(hyz, split(coarse), (0, 0))
    out[...] = result.reshape(n, n, length)
    wait_all(ret)
    out[n - 1] += got[0:n]
    out[0] += got[n : 2 * n]
    out[:, n - 1] += got[2 * n : 3 * n]
    out[:, 0] += got[3 * n : 4 * n]
    for e in range(4):
        k, j = (n - 1, 0)[e >> 1], (n - 1, 0)[e & 1]
        out[k, j : j + 1] += got[4 * n + e : 4 * n + e + 1]


def per_device(sizes, residual, local_stream, local_normal, local_span, eigen_stream, eigen_normal,
               eigen_span, vertex_stream, vertex_normal, vertex_span, level_stream, level_normal,
               level_span):
    nx, ny, nz = sizes
    block = local_stream.shape[0]
    n = block - 2
    length = residual.shape[2]
    rows = n * n + 4 * n + 16
    lanes = -(-block * block // 128) * 128
    mn = ny * nz
    copies = 18 + nx + ny + nz - 3
    vmem = pl.BlockSpec(memory_space=pltpu.VMEM)
    return pl.pallas_call(
        functools.partial(kernel, sizes),
        out_shape=jax.ShapeDtypeStruct(residual.shape, F32),
        in_specs=[vmem] * 13,
        out_specs=vmem,
        scratch_shapes=[
            pltpu.VMEM((rows - n * n, length), F32),
            pltpu.VMEM((rows, lanes), BF16),
            pltpu.VMEM((rows, lanes), BF16),
            pltpu.VMEM((length + 2 * HALO, lanes), F32),
            pltpu.VMEM((rows - n * n, length), F32),
            pltpu.VMEM((rows - n * n, length), F32),
            pltpu.VMEM((nx + ny + nz - 3, mn, 128), F32),
            pltpu.VMEM((3, mn, 128), F32),
            pltpu.SemaphoreType.DMA((copies,)),
            pltpu.SemaphoreType.DMA((copies,)),
        ],
        compiler_params=pltpu.CompilerParams(collective_id=0, has_side_effects=True),
    )(
        residual, local_stream, local_normal, local_span, eigen_stream.reshape(1, -1), eigen_normal,
        eigen_span.reshape(1, -1), vertex_stream, vertex_normal, vertex_span,
        level_stream.reshape(1, -1), level_normal.reshape(1, -1), level_span.reshape(1, -1),
    )


def solution(mesh):
    sizes = (mesh.shape["ex"], mesh.shape["ey"], mesh.shape["ez"])
    placed = (P("ez", "ey", "ex"), P(), P("ey", None, None), P(), P(), P("ey", None)) + (P(),) * 7
    return jax.shard_map(
        functools.partial(per_device, sizes), mesh=mesh, in_specs=placed,
        out_specs=P("ez", "ey", "ex"), check_vma=False,
    )
```

```python
import functools
import math

import jax
import jax.numpy as jnp
from jax import lax
from jax.experimental import pallas as pl
from jax.experimental.pallas import tpu as pltpu
from jax.sharding import PartitionSpec as P

F32 = jnp.float32
BF16 = jnp.bfloat16
I32 = jnp.int32
HALO = 24
DIRS = ((1, 0), (-1, 0), (0, 1), (0, -1), (1, 1), (1, -1), (-1, 1), (-1, -1))


def iota(shape, dim):
    return lax.broadcasted_iota(I32, shape, dim)


def quotient(x, d):
    return (x * (65536 // d + 1)) >> 16


def onehot(mask):
    return jnp.where(mask, 1.0, 0.0).astype(F32)


def split(x):
    hi = x.astype(BF16)
    return hi, (x - hi.astype(F32)).astype(BF16)


def dg(a, b, dims):
    return lax.dot_general(a, b, ((dims[:1], dims[1:]), ((), ())), preferred_element_type=F32)


def dot3(a, b, dims=(1, 0)):
    (ah, al), (bh, bl) = a, b
    return dg(ah, bh, dims) + (dg(ah, bl, dims) + dg(al, bh, dims))


def pick(mask, values, dims=(1, 0)):
    hi, lo = split(values)
    mask = mask.astype(BF16)
    return dg(mask, hi, dims) + dg(mask, lo, dims)


def hat(index, points):
    out = jnp.zeros(index.shape, F32)
    for i in range(points):
        out = jnp.where(index == i, (1.0 - math.cos(math.pi * i / (points - 1))) / 2.0, out)
    return out


def kernel(
    sizes,
    *refs,
):
    inputs, out = refs[:13], refs[13]
    rim, kh, kl, cx, back, got, parts, mine, ssem, rsem, isem = refs[14:25]
    held = refs[25:]
    (
        res, stream, normal, span, eig_x, eig_y, eig_z,
        v_stream, v_normal, v_span, lev_x, lev_y, lev_z,
    ) = held
    for i in range(13):
        pltpu.make_async_copy(inputs[i], held[i], isem.at[i]).start()
    nx, ny, nz = sizes
    block = stream.shape[0]
    n = block - 2
    sh = n.bit_length() - 1
    length = res.shape[2]
    ne = length // n
    main = n * n
    rows = kh.shape[0]
    nrim = rows - main
    lanes = kh.shape[1]
    edge = main + 4 * n
    nv, nm = v_stream.shape
    mn = nz * ny
    ix, iy, iz = lax.axis_index("ex"), lax.axis_index("ey"), lax.axis_index("ez")

    rim[...] = jnp.zeros_like(rim)
    got[...] = jnp.zeros_like(got)

    def wrap(i, size):
        return lax.rem(i + size, size)

    def has(dy):
        return jnp.logical_and(iy + dy >= 0, iy + dy < ny)

    def guarded(dy, fn):
        if dy == 0:
            fn()
        else:
            pl.when(has(dy))(fn)

    barrier = pltpu.get_barrier_semaphore()

    def signal(where):
        pl.semaphore_signal(
            barrier, inc=1, device_id=where, device_id_type=pl.DeviceIdType.MESH
        )

    for axis, index, size in (("ez", iz, nz), ("ey", iy, ny), ("ex", ix, nx)):
        for d in range(1, size):
            signal({axis: lax.rem(index + d, size)})
    for dz, dy in DIRS[4:]:
        guarded(dy, functools.partial(signal, {"ez": wrap(iz + dz, nz), "ey": iy + dy}))
    inner = jnp.where(iy > 0, 2, 0) + jnp.where(iy < ny - 1, 2, 0)

    for i in range(13):
        pltpu.make_async_copy(inputs[i], held[i], isem.at[i]).wait()
    data = res[...].reshape(main, length)
    row, col = iota((rows, block), 0), iota((rows, block), 1)
    low = row & (n - 1)
    e0 = row - edge
    rk = jnp.where(row < main, (row >> sh) + 1, low + 1)
    rk = jnp.where((row >= main) & (row < main + n), 0, rk)
    rk = jnp.where((row >= main + n) & (row < main + 2 * n), n + 1, rk)
    rk = jnp.where(row >= edge, jnp.where(e0 < 2, 0, n + 1), rk)
    rk = jnp.where(row >= edge + 4, -1, rk)
    rj = jnp.where((row >= main + 2 * n) & (row < main + 3 * n), 0, low + 1)
    rj = jnp.where((row >= main + 3 * n) & (row < main + 4 * n), n + 1, rj)
    rj = jnp.where(row >= edge, jnp.where((e0 & 1) == 0, 0, n + 1), rj)
    rj = jnp.where(row >= edge + 4, -1, rj)
    sel_k, sel_j = onehot(rk == col), onehot(rj == col)
    brow, bcol = iota((block, lanes), 0), iota((block, lanes), 1)
    bq = quotient(bcol, block)
    to_r = onehot(bq == brow)
    to_q = onehot((bcol - block * bq == brow) & (bcol < block * block))
    span_l = dot3(split(span[...]), split(to_r))
    normal_l = dot3(split(normal[...].reshape(block, block)), split(to_q))
    kmat = pick(sel_k, span_l) * pick(sel_j, normal_l)
    k_hi, k_lo = split(kmat)
    kh[...] = k_hi
    kl[...] = k_lo

    wn = n
    hrow, hcol = iota((8, main), 0), iota((8, main), 1)
    wk, wj = hat(hcol >> sh, wn), hat(hcol & (n - 1), wn)
    hyz = jnp.where((hrow & 2) > 0, wk, 1.0 - wk) * jnp.where((hrow & 1) > 0, wj, 1.0 - wj)
    hyz = split(jnp.where(hrow < 4, hyz, 0.0))
    xrow, xcol = iota((length, nv), 0), iota((length, nv), 1)
    wx = hat(xrow & (n - 1), wn)
    base = ix * ne + (xrow >> sh)
    after = jnp.where(base + 1 >= nv, base + 1 - nv, base + 1)
    hx = jnp.where(xcol == base, 1.0 - wx, 0.0) + jnp.where(xcol == after, wx, 0.0)
    wxm = split(dot3(split(hx), split(v_stream[...])))
    d_split = split(data)
    loads = dot3(split(dot3(hyz, d_split)), wxm)
    mrow, mcol = iota((mn, nz), 0), iota((mn, nz), 1)
    is_m = onehot((mrow >= mcol * ny) & (mrow < (mcol + 1) * ny))
    nrow, ncol = iota((mn, ny), 0), iota((mn, ny), 1)
    is_n = onehot(nrow - ny * quotient(nrow, ny) == ncol)
    vrow, vcol = iota((nz, 8), 0), iota((nz, 8), 1)
    vz = iz + (vcol >> 1)
    vz = jnp.where(vz >= nz, vz - nz, vz)
    at_z = onehot((vrow == vz) & (vcol < 4))
    urow, ucol = iota((ny, 8), 0), iota((ny, 8), 1)
    at_y = onehot((urow == iy + (ucol & 1)) & (ucol < 4))
    amat = pick(is_m, dot3(split(v_span[...].T), split(at_z)))
    amat = amat * pick(is_n, dot3(split(v_normal[...].T), split(at_y)))
    a_split = split(amat)
    mine[0, :, :nm] = dot3(a_split, split(loads))
    level = jnp.sum(is_m * lev_z[...], axis=1, keepdims=True)
    level = level + jnp.sum(is_n * lev_y[...], axis=1, keepdims=True) + lev_x[...]

    pl.semaphore_wait(barrier, (nx - 1) + (ny - 1) + (nz - 1) + inner)

    def shipped(src, dst, slot, where):
        return pltpu.make_async_remote_copy(
            src_ref=src, dst_ref=dst, send_sem=ssem.at[slot], recv_sem=rsem.at[slot],
            device_id=where, device_id_type=pl.DeviceIdType.MESH,
        )

    def target(dz, dy):
        where = {}
        if dz:
            where["ez"] = wrap(iz + dz, nz)
        if dy:
            where["ey"] = iy + dy
        return where

    def halo(slot):
        dz, dy = DIRS[slot]
        if dy == 0:
            src = res.at[n - 1 if dz > 0 else 0]
            dst = rim.at[pl.ds(0 if dz > 0 else n, n)]
        elif dz == 0:
            src = res.at[:, n - 1 if dy > 0 else 0]
            dst = rim.at[pl.ds(2 * n if dy > 0 else 3 * n, n)]
        else:
            src = res.at[n - 1 if dz > 0 else 0, pl.ds(n - 1 if dy > 0 else 0, 1)]
            dst = rim.at[pl.ds(4 * n + (0 if dz > 0 else 2) + (0 if dy > 0 else 1), 1)]
        return shipped(src, dst, slot, target(dz, dy))

    def ret(slot):
        dz, dy = DIRS[slot]
        if dy == 0:
            at, number = (n if dz > 0 else 0), n
        elif dz == 0:
            at, number = (3 * n if dy > 0 else 2 * n), n
        else:
            at, number = 4 * n + (2 if dz > 0 else 0) + (1 if dy > 0 else 0), 1
        return shipped(
            back.at[pl.ds(at, number)], got.at[pl.ds(at, number)], 8 + slot, target(dz, dy)
        )

    def start_all(make):
        for s, (dz, dy) in enumerate(DIRS):
            guarded(dy, lambda s=s: make(s).start())

    def wait_all(make):
        for s, (dz, dy) in enumerate(DIRS):
            guarded(dy, lambda s=s: make(s).wait_send())
            guarded(-dy, lambda s=s: make(s).wait_recv())

    stages = {"ez": (0, iz, nz), "ex": (1, ix, nx), "ey": (2, iy, ny)}
    offset = {"ez": 0, "ex": nz - 1, "ey": nz + nx - 2}

    def stage_copies(axis):
        st, index, size = stages[axis]
        return [
            shipped(
                mine.at[st], parts.at[offset[axis] + d - 1], 18 + offset[axis] + d - 1,
                {axis: lax.rem(index + d, size)},
            )
            for d in range(1, size)
        ]

    def stage_start(axis):
        for c in stage_copies(axis):
            c.start()

    def stage_end(axis):
        st, index, size = stages[axis]
        total = mine[st, :, :nm]
        for d, c in enumerate(stage_copies(axis)):
            c.wait_recv()
            c.wait_send()
            total = total + parts[offset[axis] + d, :, :nm]
        return total

    start_all(halo)
    stage_start("ez")
    k_main = kh[0:main], kl[0:main]
    k_rim = kh[main:], kl[main:]
    c_main = dot3(split(data.T), k_main)
    nep = cx.shape[0]
    pairs = (ne + 2) * block
    npad = -(-pairs // 16) * 16
    wrow, wcol = iota((npad, nep), 0), iota((npad, nep), 1)
    xs = jnp.where(wcol < length, wcol, jnp.where(wcol < length + HALO, wcol - length - HALO, wcol - HALO))
    xi = xs + 1 + n - n * quotient(wrow, block)
    trow, tcol = iota((block, nep), 0), iota((block, nep), 1)
    tx = jnp.where(tcol < length, tcol, jnp.where(tcol < length + HALO, tcol - length - HALO, tcol - HALO))
    tm = (tx + 1) & (n - 1)
    s_t = split(stream[...].T)
    first = dot3(s_t, split(onehot(trow == tm)))
    second = dot3(s_t, split(onehot(trow - n == tm)))
    prow, pcol = iota((npad, block), 0), iota((npad, block), 1)
    is_p = onehot((prow - block * quotient(prow, block) == pcol) & (prow < pairs))
    wmat = jnp.where((xi >= 0) & (xi < n), pick(is_p, first), 0.0)
    wmat = wmat + jnp.where((xi >= n) & (xi < block), pick(is_p, second), 0.0)
    w_main = split(wmat[:, :length])
    w_halo = split(wmat[:, length:])
    w_back = split(wmat[:, :length].T)
    eig_yz = dot3(split(jnp.broadcast_to(eig_z[...], (8, block))), split(to_r))
    eig_yz = eig_yz + dot3(split(jnp.broadcast_to(eig_y[...], (8, block))), split(to_q))
    ecol = jnp.sum(is_p * eig_x[...], axis=1, keepdims=True)
    ecol = jnp.where(iota((npad, 1), 0) < pairs, ecol, 1.0)
    inverse = 1.0 / (ecol + eig_yz[0:1])

    wait_all(halo)
    cx[0:length] = c_main + dot3(split(rim[...].T), k_rim)

    def x_copies():
        right = {"ex": wrap(ix + 1, nx)}
        left = {"ex": wrap(ix - 1, nx)}
        return (
            shipped(cx.at[pl.ds(length - HALO, HALO)], cx.at[pl.ds(length, HALO)], 16, right),
            shipped(cx.at[pl.ds(0, HALO)], cx.at[pl.ds(length + HALO, HALO)], 17, left),
        )

    for c in x_copies():
        c.start()
    mine[1, :, :nm] = stage_end("ez")
    stage_start("ex")
    modal = dot3(w_main, split(cx[0:length]))
    for c in x_copies():
        c.wait()
    modal = modal + dot3(w_halo, split(cx[length:]))
    u = split(dot3(w_back, split(modal * inverse)))
    back[...] = dot3(k_rim, u, (1, 1))
    start_all(ret)
    mine[2, :, :nm] = stage_end("ex")
    stage_start("ey")
    result = dot3(k_main, u, (1, 1))
    scaled = split(stage_end("ey") / level)
    coarse = dot3(split(amat.T), scaled)
    coarse = dot3(split(coarse), wxm, (1, 1))
    result = result + dot3(hyz, split(coarse), (0, 0))
    out[...] = result.reshape(n, n, length)
    wait_all(ret)
    out[n - 1] += got[0:n]
    out[0] += got[n : 2 * n]
    out[:, n - 1] += got[2 * n : 3 * n]
    out[:, 0] += got[3 * n : 4 * n]
    for e in range(4):
        k, j = (n - 1, 0)[e >> 1], (n - 1, 0)[e & 1]
        out[k, j : j + 1] += got[4 * n + e : 4 * n + e + 1]


def per_device(sizes, residual, local_stream, local_normal, local_span, eigen_stream, eigen_normal,
               eigen_span, vertex_stream, vertex_normal, vertex_span, level_stream, level_normal,
               level_span):
    nx, ny, nz = sizes
    block = local_stream.shape[0]
    n = block - 2
    length = residual.shape[2]
    rows = n * n + 4 * n + 16
    lanes = -(-block * block // 128) * 128
    mn = ny * nz
    copies = 18 + nx + ny + nz - 3
    vmem = pl.BlockSpec(memory_space=pltpu.VMEM)
    args = (
        residual, local_stream, local_normal.transpose(1, 0, 2), local_span,
        eigen_stream.reshape(1, -1), eigen_normal, eigen_span.reshape(1, -1), vertex_stream,
        vertex_normal, vertex_span, level_stream.reshape(1, -1), level_normal.reshape(1, -1),
        level_span.reshape(1, -1),
    )
    return pl.pallas_call(
        functools.partial(kernel, sizes),
        out_shape=pltpu.VMEM(residual.shape, F32),
        in_specs=[pl.BlockSpec(memory_space=pltpu.HBM)] * 13,
        out_specs=vmem,
        scratch_shapes=[
            pltpu.VMEM((rows - n * n, length), F32),
            pltpu.VMEM((rows, lanes), BF16),
            pltpu.VMEM((rows, lanes), BF16),
            pltpu.VMEM((length + 2 * HALO, lanes), F32),
            pltpu.VMEM((rows - n * n, length), F32),
            pltpu.VMEM((rows - n * n, length), F32),
            pltpu.VMEM((nx + ny + nz - 3, mn, 128), F32),
            pltpu.VMEM((3, mn, 128), F32),
            pltpu.SemaphoreType.DMA((copies,)),
            pltpu.SemaphoreType.DMA((copies,)),
            pltpu.SemaphoreType.DMA((13,)),
        ] + [pltpu.VMEM(a.shape, F32) for a in args],
        compiler_params=pltpu.CompilerParams(
            collective_id=0, has_side_effects=True
        ),
    )(*args)


def solution(mesh):
    sizes = (mesh.shape["ex"], mesh.shape["ey"], mesh.shape["ez"])
    placed = (P("ez", "ey", "ex"), P(), P("ey", None, None), P(), P(), P("ey", None)) + (P(),) * 7
    return jax.shard_map(
        functools.partial(per_device, sizes), mesh=mesh, in_specs=placed,
        out_specs=P("ez", "ey", "ex"), check_vma=False,
    )
```

```python
import functools
import math

import jax
import jax.numpy as jnp
from jax import lax
from jax.experimental import pallas as pl
from jax.experimental.pallas import tpu as pltpu
from jax.sharding import PartitionSpec as P

F32 = jnp.float32
BF16 = jnp.bfloat16
I32 = jnp.int32
DIRS = ((1, 0), (-1, 0), (0, 1), (0, -1), (1, 1), (1, -1), (-1, 1), (-1, -1))


def iota(shape, dim):
    return lax.broadcasted_iota(I32, shape, dim)


def quotient(x, d):
    return (x * (65536 // d + 1)) >> 16


def onehot(mask):
    return jnp.where(mask, 1.0, 0.0).astype(F32)


def split(x):
    hi = x.astype(BF16)
    return hi, (x - hi.astype(F32)).astype(BF16)


def dg(a, b, dims):
    return lax.dot_general(a, b, ((dims[:1], dims[1:]), ((), ())), preferred_element_type=F32)


def dot3(a, b, dims=(1, 0)):
    (ah, al), (bh, bl) = a, b
    return dg(ah, bh, dims) + (dg(ah, bl, dims) + dg(al, bh, dims))


def pick(mask, values, dims=(1, 0)):
    hi, lo = split(values)
    mask = mask.astype(BF16)
    return dg(mask, hi, dims) + dg(mask, lo, dims)


def hat(index, points):
    out = jnp.zeros(index.shape, F32)
    for i in range(points):
        out = jnp.where(index == i, (1.0 - math.cos(math.pi * i / (points - 1))) / 2.0, out)
    return out


def kernel(
    sizes,
    *refs,
):
    inputs, out = refs[:13], refs[13]
    rim, kh, kl, cx, back, got, parts, mine, hx, vs, vr, us, ssem, rsem, isem = refs[14:29]
    held = refs[29:]
    (
        res, stream, normal, span, eig_x, eig_y, eig_z,
        v_stream, v_normal, v_span, lev_x, lev_y, lev_z,
    ) = held
    for i in range(13):
        pltpu.make_async_copy(inputs[i], held[i], isem.at[i]).start()
    nx, ny, nz = sizes
    block = stream.shape[0]
    n = block - 2
    sh = n.bit_length() - 1
    length = res.shape[2]
    ne = length // n
    main = n * n
    rows = kh.shape[0]
    nrim = rows - main
    lanes = kh.shape[1]
    edge = main + 4 * n
    nv, nm = v_stream.shape
    mn = nz * ny
    ix, iy, iz = lax.axis_index("ex"), lax.axis_index("ey"), lax.axis_index("ez")

    rim[...] = jnp.zeros_like(rim)
    got[...] = jnp.zeros_like(got)
    hx[...] = jnp.zeros_like(hx)

    def wrap(i, size):
        return lax.rem(i + size, size)

    def has(dy):
        return jnp.logical_and(iy + dy >= 0, iy + dy < ny)

    def guarded(dy, fn):
        if dy == 0:
            fn()
        else:
            pl.when(has(dy))(fn)

    barrier = pltpu.get_barrier_semaphore()

    def signal(where):
        pl.semaphore_signal(
            barrier, inc=1, device_id=where, device_id_type=pl.DeviceIdType.MESH
        )

    for axis, index, size in (("ez", iz, nz), ("ey", iy, ny), ("ex", ix, nx)):
        for d in range(1, size):
            signal({axis: lax.rem(index + d, size)})
    for dz, dy in DIRS[4:]:
        guarded(dy, functools.partial(signal, {"ez": wrap(iz + dz, nz), "ey": iy + dy}))
    inner = jnp.where(iy > 0, 2, 0) + jnp.where(iy < ny - 1, 2, 0)

    for i in range(13):
        pltpu.make_async_copy(inputs[i], held[i], isem.at[i]).wait()
    data = res[...].reshape(main, length)
    row, col = iota((rows, block), 0), iota((rows, block), 1)
    low = row & (n - 1)
    e0 = row - edge
    rk = jnp.where(row < main, (row >> sh) + 1, low + 1)
    rk = jnp.where((row >= main) & (row < main + n), 0, rk)
    rk = jnp.where((row >= main + n) & (row < main + 2 * n), n + 1, rk)
    rk = jnp.where(row >= edge, jnp.where(e0 < 2, 0, n + 1), rk)
    rk = jnp.where(row >= edge + 4, -1, rk)
    rj = jnp.where((row >= main + 2 * n) & (row < main + 3 * n), 0, low + 1)
    rj = jnp.where((row >= main + 3 * n) & (row < main + 4 * n), n + 1, rj)
    rj = jnp.where(row >= edge, jnp.where((e0 & 1) == 0, 0, n + 1), rj)
    rj = jnp.where(row >= edge + 4, -1, rj)
    sel_k, sel_j = onehot(rk == col), onehot(rj == col)
    brow, bcol = iota((block, lanes), 0), iota((block, lanes), 1)
    bq = quotient(bcol, block)
    to_r = onehot(bq == brow)
    to_q = onehot((bcol - block * bq == brow) & (bcol < block * block))
    span_l = dot3(split(span[...]), split(to_r))
    normal_l = dot3(split(normal[...].reshape(block, block)), split(to_q))
    kmat = pick(sel_k, span_l) * pick(sel_j, normal_l)
    k_hi, k_lo = split(kmat)
    kh[...] = k_hi
    kl[...] = k_lo

    wn = n
    hrow, hcol = iota((8, main), 0), iota((8, main), 1)
    wk, wj = hat(hcol >> sh, wn), hat(hcol & (n - 1), wn)
    hyz = jnp.where((hrow & 2) > 0, wk, 1.0 - wk) * jnp.where((hrow & 1) > 0, wj, 1.0 - wj)
    hyz = split(jnp.where(hrow < 4, hyz, 0.0))
    xrow, xcol = iota((length, nv), 0), iota((length, nv), 1)
    wx = hat(xrow & (n - 1), wn)
    base = ix * ne + (xrow >> sh)
    after = jnp.where(base + 1 >= nv, base + 1 - nv, base + 1)
    hatx = jnp.where(xcol == base, 1.0 - wx, 0.0) + jnp.where(xcol == after, wx, 0.0)
    wxm = split(dot3(split(hatx), split(v_stream[...])))
    d_split = split(data)
    loads = dot3(split(dot3(hyz, d_split)), wxm)
    mrow, mcol = iota((mn, nz), 0), iota((mn, nz), 1)
    is_m = onehot((mrow >= mcol * ny) & (mrow < (mcol + 1) * ny))
    nrow, ncol = iota((mn, ny), 0), iota((mn, ny), 1)
    is_n = onehot(nrow - ny * quotient(nrow, ny) == ncol)
    vrow, vcol = iota((nz, 8), 0), iota((nz, 8), 1)
    vz = iz + (vcol >> 1)
    vz = jnp.where(vz >= nz, vz - nz, vz)
    at_z = onehot((vrow == vz) & (vcol < 4))
    urow, ucol = iota((ny, 8), 0), iota((ny, 8), 1)
    at_y = onehot((urow == iy + (ucol & 1)) & (ucol < 4))
    amat = pick(is_m, dot3(split(v_span[...].T), split(at_z)))
    amat = amat * pick(is_n, dot3(split(v_normal[...].T), split(at_y)))
    a_split = split(amat)
    mine[0, :, :nm] = dot3(a_split, split(loads))
    level = jnp.sum(is_m * lev_z[...], axis=1, keepdims=True)
    level = level + jnp.sum(is_n * lev_y[...], axis=1, keepdims=True) + lev_x[...]

    pl.semaphore_wait(barrier, (nx - 1) + (ny - 1) + (nz - 1) + inner)

    def shipped(src, dst, slot, where):
        return pltpu.make_async_remote_copy(
            src_ref=src, dst_ref=dst, send_sem=ssem.at[slot], recv_sem=rsem.at[slot],
            device_id=where, device_id_type=pl.DeviceIdType.MESH,
        )

    def target(dz, dy):
        where = {}
        if dz:
            where["ez"] = wrap(iz + dz, nz)
        if dy:
            where["ey"] = iy + dy
        return where

    def halo(slot):
        dz, dy = DIRS[slot]
        if dy == 0:
            src = res.at[n - 1 if dz > 0 else 0]
            dst = rim.at[pl.ds(0 if dz > 0 else n, n)]
        elif dz == 0:
            src = res.at[:, n - 1 if dy > 0 else 0]
            dst = rim.at[pl.ds(2 * n if dy > 0 else 3 * n, n)]
        else:
            src = res.at[n - 1 if dz > 0 else 0, pl.ds(n - 1 if dy > 0 else 0, 1)]
            dst = rim.at[pl.ds(4 * n + (0 if dz > 0 else 2) + (0 if dy > 0 else 1), 1)]
        return shipped(src, dst, slot, target(dz, dy))

    def ret(slot):
        dz, dy = DIRS[slot]
        if dy == 0:
            at, number = (n if dz > 0 else 0), n
        elif dz == 0:
            at, number = (3 * n if dy > 0 else 2 * n), n
        else:
            at, number = 4 * n + (2 if dz > 0 else 0) + (1 if dy > 0 else 0), 1
        return shipped(
            back.at[pl.ds(at, number)], got.at[pl.ds(at, number)], 8 + slot, target(dz, dy)
        )

    def start_all(make):
        for s, (dz, dy) in enumerate(DIRS):
            guarded(dy, lambda s=s: make(s).start())

    def wait_all(make):
        for s, (dz, dy) in enumerate(DIRS):
            guarded(dy, lambda s=s: make(s).wait_send())
            guarded(-dy, lambda s=s: make(s).wait_recv())

    stages = {"ez": (0, iz, nz), "ex": (1, ix, nx), "ey": (2, iy, ny)}
    offset = {"ez": 0, "ex": nz - 1, "ey": nz + nx - 2}

    def stage_copies(axis):
        st, index, size = stages[axis]
        return [
            shipped(
                mine.at[st], parts.at[offset[axis] + d - 1], 20 + offset[axis] + d - 1,
                {axis: lax.rem(index + d, size)},
            )
            for d in range(1, size)
        ]

    def stage_start(axis):
        for c in stage_copies(axis):
            c.start()

    def stage_end(axis):
        st, index, size = stages[axis]
        total = mine[st, :, :nm]
        for d, c in enumerate(stage_copies(axis)):
            c.wait_recv()
            c.wait_send()
            total = total + parts[offset[axis] + d, :, :nm]
        return total

    start_all(halo)
    stage_start("ez")
    k_main = kh[0:main], kl[0:main]
    k_rim = kh[main:], kl[main:]
    c_main = dot3(split(data.T), k_main)
    nep = length + 16
    pairs = ne * block
    npad = -(-pairs // 16) * 16

    def place(c):
        far = jnp.where(c == length + 8, length, -n * length)
        return jnp.where(c < length, c, jnp.where(c == length, -1, far))

    wrow, wcol = iota((npad, nep), 0), iota((npad, nep), 1)
    xi = place(wcol) + 1 - n * quotient(wrow, block)
    trow, tcol = iota((block, nep), 0), iota((block, nep), 1)
    tx = place(tcol)
    tm = (tx + 1) & (n - 1)
    s_t = split(stream[...].T)
    first = dot3(s_t, split(onehot(trow == tm)))
    second = dot3(s_t, split(onehot(trow - n == tm)))
    prow, pcol = iota((npad, block), 0), iota((npad, block), 1)
    is_p = onehot((prow - block * quotient(prow, block) == pcol) & (prow < pairs))
    wmat = jnp.where((xi >= 0) & (xi < n), pick(is_p, first), 0.0)
    wmat = wmat + jnp.where((xi >= n) & (xi < block), pick(is_p, second), 0.0)
    w_main = split(wmat[:, :length])
    w_halo = split(wmat[:, length:])
    w_out = wmat[:, length:].T
    w_back = split(wmat[:, :length].T)
    eig_yz = dot3(split(jnp.broadcast_to(eig_z[...], (8, block))), split(to_r))
    eig_yz = eig_yz + dot3(split(jnp.broadcast_to(eig_y[...], (8, block))), split(to_q))
    ecol = jnp.sum(is_p * eig_x[...], axis=1, keepdims=True)
    ecol = jnp.where(iota((npad, 1), 0) < pairs, ecol, 1.0)
    inverse = 1.0 / (ecol + eig_yz[0:1])
    own = dot3(split(w_out * w_out), split(inverse))
    w_out = split(w_out)

    wait_all(halo)
    cx[...] = c_main + dot3(split(rim[...].T), k_rim)

    right = {"ex": wrap(ix + 1, nx)}
    left = {"ex": wrap(ix - 1, nx)}

    def x_copies():
        return (
            shipped(cx.at[pl.ds(length - 1, 1)], hx.at[pl.ds(0, 1)], 16, right),
            shipped(cx.at[pl.ds(0, 1)], hx.at[pl.ds(8, 1)], 17, left),
        )

    def v_copies():
        return (
            shipped(vs.at[pl.ds(8, 1)], vr.at[pl.ds(0, 1)], 18, right),
            shipped(vs.at[pl.ds(0, 1)], vr.at[pl.ds(8, 1)], 19, left),
        )

    for c in x_copies():
        c.start()
    modal = dot3(w_main, split(cx[...]))
    vs[...] = dot3(w_out, split(modal * inverse))
    for c in v_copies():
        c.start()
    mine[1, :, :nm] = stage_end("ez")
    stage_start("ex")
    for c in x_copies():
        c.wait()
    modal = modal + dot3(w_halo, split(hx[...]))
    us[...] = dot3(w_back, split(modal * inverse))
    for c in v_copies():
        c.wait()
    us[0:1] += vr[0:1] + own[8:9] * cx[0:1]
    us[length - 1 : length] += vr[8:9] + own[0:1] * cx[length - 1 : length]
    u = split(us[...])
    back[...] = dot3(k_rim, u, (1, 1))
    start_all(ret)
    mine[2, :, :nm] = stage_end("ex")
    stage_start("ey")
    result = dot3(k_main, u, (1, 1))
    scaled = split(stage_end("ey") / level)
    coarse = dot3(split(amat.T), scaled)
    coarse = dot3(split(coarse), wxm, (1, 1))
    result = result + dot3(hyz, split(coarse), (0, 0))
    out[...] = result.reshape(n, n, length)
    wait_all(ret)
    out[n - 1] += got[0:n]
    out[0] += got[n : 2 * n]
    out[:, n - 1] += got[2 * n : 3 * n]
    out[:, 0] += got[3 * n : 4 * n]
    for e in range(4):
        k, j = (n - 1, 0)[e >> 1], (n - 1, 0)[e & 1]
        out[k, j : j + 1] += got[4 * n + e : 4 * n + e + 1]


def per_device(sizes, residual, local_stream, local_normal, local_span, eigen_stream, eigen_normal,
               eigen_span, vertex_stream, vertex_normal, vertex_span, level_stream, level_normal,
               level_span):
    nx, ny, nz = sizes
    block = local_stream.shape[0]
    n = block - 2
    length = residual.shape[2]
    rows = n * n + 4 * n + 16
    lanes = -(-block * block // 128) * 128
    mn = ny * nz
    copies = 20 + nx + ny + nz - 3
    vmem = pl.BlockSpec(memory_space=pltpu.VMEM)
    args = (
        residual, local_stream, local_normal.transpose(1, 0, 2), local_span,
        eigen_stream.reshape(1, -1), eigen_normal, eigen_span.reshape(1, -1), vertex_stream,
        vertex_normal, vertex_span, level_stream.reshape(1, -1), level_normal.reshape(1, -1),
        level_span.reshape(1, -1),
    )
    return pl.pallas_call(
        functools.partial(kernel, sizes),
        out_shape=pltpu.VMEM(residual.shape, F32),
        in_specs=[pl.BlockSpec(memory_space=pltpu.HBM)] * 13,
        out_specs=vmem,
        scratch_shapes=[
            pltpu.VMEM((rows - n * n, length), F32),
            pltpu.VMEM((rows, lanes), BF16),
            pltpu.VMEM((rows, lanes), BF16),
            pltpu.VMEM((length, lanes), F32),
            pltpu.VMEM((rows - n * n, length), F32),
            pltpu.VMEM((rows - n * n, length), F32),
            pltpu.VMEM((nx + ny + nz - 3, mn, 128), F32),
            pltpu.VMEM((3, mn, 128), F32),
            pltpu.VMEM((16, lanes), F32),
            pltpu.VMEM((16, lanes), F32),
            pltpu.VMEM((16, lanes), F32),
            pltpu.VMEM((length, lanes), F32),
            pltpu.SemaphoreType.DMA((copies,)),
            pltpu.SemaphoreType.DMA((copies,)),
            pltpu.SemaphoreType.DMA((13,)),
        ] + [pltpu.VMEM(a.shape, F32) for a in args],
        compiler_params=pltpu.CompilerParams(
            collective_id=0, has_side_effects=True
        ),
    )(*args)


def solution(mesh):
    sizes = (mesh.shape["ex"], mesh.shape["ey"], mesh.shape["ez"])
    placed = (P("ez", "ey", "ex"), P(), P("ey", None, None), P(), P(), P("ey", None)) + (P(),) * 7
    return jax.shard_map(
        functools.partial(per_device, sizes), mesh=mesh, in_specs=placed,
        out_specs=P("ez", "ey", "ex"), check_vma=False,
    )
```

```python
import functools
import math

import jax
import jax.numpy as jnp
from jax import lax
from jax.experimental import pallas as pl
from jax.experimental.pallas import tpu as pltpu
from jax.sharding import PartitionSpec as P

F32 = jnp.float32
BF16 = jnp.bfloat16
I32 = jnp.int32
DIRS = ((1, 0), (-1, 0), (0, 1), (0, -1), (1, 1), (1, -1), (-1, 1), (-1, -1))


def iota(shape, dim):
    return lax.broadcasted_iota(I32, shape, dim)


def quotient(x, d):
    return (x * (65536 // d + 1)) >> 16


def onehot(mask):
    return jnp.where(mask, 1.0, 0.0).astype(F32)


def split(x):
    hi = x.astype(BF16)
    return hi, (x - hi.astype(F32)).astype(BF16)


def dg(a, b, dims):
    return lax.dot_general(a, b, ((dims[:1], dims[1:]), ((), ())), preferred_element_type=F32)


def dot3(a, b, dims=(1, 0)):
    (ah, al), (bh, bl) = a, b
    return dg(ah, bh, dims) + (dg(ah, bl, dims) + dg(al, bh, dims))


def pick(mask, values, dims=(1, 0)):
    hi, lo = split(values)
    mask = mask.astype(BF16)
    return dg(mask, hi, dims) + dg(mask, lo, dims)


def hat(index, points):
    out = jnp.zeros(index.shape, F32)
    for i in range(points):
        out = jnp.where(index == i, (1.0 - math.cos(math.pi * i / (points - 1))) / 2.0, out)
    return out


def kernel(
    sizes,
    *refs,
):
    inputs, out = refs[:13], refs[13]
    rim, kh, kl, cx, back, got, parts, mine, hx, vs, vr, us, ssem, rsem, isem = refs[14:29]
    held = refs[29:]
    (
        res, stream, normal, span, eig_x, eig_y, eig_z,
        v_stream, v_normal, v_span, lev_x, lev_y, lev_z,
    ) = held
    for i in range(13):
        pltpu.make_async_copy(inputs[i], held[i], isem.at[i]).start()
    nx, ny, nz = sizes
    block = stream.shape[0]
    n = block - 2
    sh = n.bit_length() - 1
    length = res.shape[2]
    ne = length // n
    main = n * n
    rows = kh.shape[0]
    nrim = rows - main
    lanes = kh.shape[1]
    edge = main + 4 * n
    nv, nm = v_stream.shape
    mn = nz * ny
    ix, iy, iz = lax.axis_index("ex"), lax.axis_index("ey"), lax.axis_index("ez")

    rim[...] = jnp.zeros_like(rim)
    got[...] = jnp.zeros_like(got)
    hx[...] = jnp.zeros_like(hx)

    def wrap(i, size):
        return lax.rem(i + size, size)

    def has(dy):
        return jnp.logical_and(iy + dy >= 0, iy + dy < ny)

    def guarded(dy, fn):
        if dy == 0:
            fn()
        else:
            pl.when(has(dy))(fn)

    barrier = pltpu.get_barrier_semaphore()

    def signal(where):
        pl.semaphore_signal(
            barrier, inc=1, device_id=where, device_id_type=pl.DeviceIdType.MESH
        )

    for axis, index, size in (("ez", iz, nz), ("ey", iy, ny), ("ex", ix, nx)):
        for d in range(1, size):
            signal({axis: lax.rem(index + d, size)})
    for dz, dy in DIRS[4:]:
        guarded(dy, functools.partial(signal, {"ez": wrap(iz + dz, nz), "ey": iy + dy}))
    inner = jnp.where(iy > 0, 2, 0) + jnp.where(iy < ny - 1, 2, 0)

    pltpu.make_async_copy(inputs[0], held[0], isem.at[0]).wait()
    pl.semaphore_wait(barrier, (nx - 1) + (ny - 1) + (nz - 1) + inner)

    def shipped(src, dst, slot, where):
        return pltpu.make_async_remote_copy(
            src_ref=src, dst_ref=dst, send_sem=ssem.at[slot], recv_sem=rsem.at[slot],
            device_id=where, device_id_type=pl.DeviceIdType.MESH,
        )

    def target(dz, dy):
        where = {}
        if dz:
            where["ez"] = wrap(iz + dz, nz)
        if dy:
            where["ey"] = iy + dy
        return where

    def halo(slot):
        dz, dy = DIRS[slot]
        if dy == 0:
            src = res.at[n - 1 if dz > 0 else 0]
            dst = rim.at[pl.ds(0 if dz > 0 else n, n)]
        elif dz == 0:
            src = res.at[:, n - 1 if dy > 0 else 0]
            dst = rim.at[pl.ds(2 * n if dy > 0 else 3 * n, n)]
        else:
            src = res.at[n - 1 if dz > 0 else 0, pl.ds(n - 1 if dy > 0 else 0, 1)]
            dst = rim.at[pl.ds(4 * n + (0 if dz > 0 else 2) + (0 if dy > 0 else 1), 1)]
        return shipped(src, dst, slot, target(dz, dy))

    def ret(slot):
        dz, dy = DIRS[slot]
        if dy == 0:
            at, number = (n if dz > 0 else 0), n
        elif dz == 0:
            at, number = (3 * n if dy > 0 else 2 * n), n
        else:
            at, number = 4 * n + (2 if dz > 0 else 0) + (1 if dy > 0 else 0), 1
        return shipped(
            back.at[pl.ds(at, number)], got.at[pl.ds(at, number)], 8 + slot, target(dz, dy)
        )

    def start_all(make):
        for s, (dz, dy) in enumerate(DIRS):
            guarded(dy, lambda s=s: make(s).start())

    def wait_all(make):
        for s, (dz, dy) in enumerate(DIRS):
            guarded(dy, lambda s=s: make(s).wait_send())
            guarded(-dy, lambda s=s: make(s).wait_recv())

    stages = {"ez": (0, iz, nz), "ex": (1, ix, nx), "ey": (2, iy, ny)}
    offset = {"ez": 0, "ex": nz - 1, "ey": nz + nx - 2}

    def stage_copies(axis):
        st, index, size = stages[axis]
        return [
            shipped(
                mine.at[st], parts.at[offset[axis] + d - 1], 20 + offset[axis] + d - 1,
                {axis: lax.rem(index + d, size)},
            )
            for d in range(1, size)
        ]

    def stage_start(axis):
        for c in stage_copies(axis):
            c.start()

    def stage_end(axis):
        st, index, size = stages[axis]
        total = mine[st, :, :nm]
        for d, c in enumerate(stage_copies(axis)):
            c.wait_recv()
            c.wait_send()
            total = total + parts[offset[axis] + d, :, :nm]
        return total

    start_all(halo)
    for i in range(1, 13):
        pltpu.make_async_copy(inputs[i], held[i], isem.at[i]).wait()
    data = res[...].reshape(main, length)
    row, col = iota((rows, block), 0), iota((rows, block), 1)
    low = row & (n - 1)
    e0 = row - edge
    rk = jnp.where(row < main, (row >> sh) + 1, low + 1)
    rk = jnp.where((row >= main) & (row < main + n), 0, rk)
    rk = jnp.where((row >= main + n) & (row < main + 2 * n), n + 1, rk)
    rk = jnp.where(row >= edge, jnp.where(e0 < 2, 0, n + 1), rk)
    rk = jnp.where(row >= edge + 4, -1, rk)
    rj = jnp.where((row >= main + 2 * n) & (row < main + 3 * n), 0, low + 1)
    rj = jnp.where((row >= main + 3 * n) & (row < main + 4 * n), n + 1, rj)
    rj = jnp.where(row >= edge, jnp.where((e0 & 1) == 0, 0, n + 1), rj)
    rj = jnp.where(row >= edge + 4, -1, rj)
    sel_k, sel_j = onehot(rk == col), onehot(rj == col)
    brow, bcol = iota((block, lanes), 0), iota((block, lanes), 1)
    bq = quotient(bcol, block)
    to_r = onehot(bq == brow)
    to_q = onehot((bcol - block * bq == brow) & (bcol < block * block))
    span_l = dot3(split(span[...]), split(to_r))
    normal_l = dot3(split(normal[...].reshape(block, block)), split(to_q))
    kmat = pick(sel_k, span_l) * pick(sel_j, normal_l)
    k_hi, k_lo = split(kmat)
    kh[...] = k_hi
    kl[...] = k_lo

    wn = n
    hrow, hcol = iota((8, main), 0), iota((8, main), 1)
    wk, wj = hat(hcol >> sh, wn), hat(hcol & (n - 1), wn)
    hyz = jnp.where((hrow & 2) > 0, wk, 1.0 - wk) * jnp.where((hrow & 1) > 0, wj, 1.0 - wj)
    hyz = split(jnp.where(hrow < 4, hyz, 0.0))
    xrow, xcol = iota((length, nv), 0), iota((length, nv), 1)
    wx = hat(xrow & (n - 1), wn)
    base = ix * ne + (xrow >> sh)
    after = jnp.where(base + 1 >= nv, base + 1 - nv, base + 1)
    hatx = jnp.where(xcol == base, 1.0 - wx, 0.0) + jnp.where(xcol == after, wx, 0.0)
    wxm = split(dot3(split(hatx), split(v_stream[...])))
    d_split = split(data)
    loads = dot3(split(dot3(hyz, d_split)), wxm)
    mrow, mcol = iota((mn, nz), 0), iota((mn, nz), 1)
    is_m = onehot((mrow >= mcol * ny) & (mrow < (mcol + 1) * ny))
    nrow, ncol = iota((mn, ny), 0), iota((mn, ny), 1)
    is_n = onehot(nrow - ny * quotient(nrow, ny) == ncol)
    vrow, vcol = iota((nz, 8), 0), iota((nz, 8), 1)
    vz = iz + (vcol >> 1)
    vz = jnp.where(vz >= nz, vz - nz, vz)
    at_z = onehot((vrow == vz) & (vcol < 4))
    urow, ucol = iota((ny, 8), 0), iota((ny, 8), 1)
    at_y = onehot((urow == iy + (ucol & 1)) & (ucol < 4))
    amat = pick(is_m, dot3(split(v_span[...].T), split(at_z)))
    amat = amat * pick(is_n, dot3(split(v_normal[...].T), split(at_y)))
    a_split = split(amat)
    mine[0, :, :nm] = dot3(a_split, split(loads))
    level = jnp.sum(is_m * lev_z[...], axis=1, keepdims=True)
    level = level + jnp.sum(is_n * lev_y[...], axis=1, keepdims=True) + lev_x[...]

    stage_start("ez")
    k_main = kh[0:main], kl[0:main]
    k_rim = kh[main:], kl[main:]
    c_main = dot3(split(data.T), k_main)
    nep = length + 16
    pairs = ne * block
    npad = -(-pairs // 16) * 16

    def place(c):
        far = jnp.where(c == length + 8, length, -n * length)
        return jnp.where(c < length, c, jnp.where(c == length, -1, far))

    wrow, wcol = iota((npad, nep), 0), iota((npad, nep), 1)
    xi = place(wcol) + 1 - n * quotient(wrow, block)
    trow, tcol = iota((block, nep), 0), iota((block, nep), 1)
    tx = place(tcol)
    tm = (tx + 1) & (n - 1)
    s_t = split(stream[...].T)
    first = dot3(s_t, split(onehot(trow == tm)))
    second = dot3(s_t, split(onehot(trow - n == tm)))
    prow, pcol = iota((npad, block), 0), iota((npad, block), 1)
    is_p = onehot((prow - block * quotient(prow, block) == pcol) & (prow < pairs))
    wmat = jnp.where((xi >= 0) & (xi < n), pick(is_p, first), 0.0)
    wmat = wmat + jnp.where((xi >= n) & (xi < block), pick(is_p, second), 0.0)
    w_main = split(wmat[:, :length])
    w_halo = split(wmat[:, length:])
    w_out = wmat[:, length:].T
    w_back = split(wmat[:, :length].T)
    eig_yz = dot3(split(jnp.broadcast_to(eig_z[...], (8, block))), split(to_r))
    eig_yz = eig_yz + dot3(split(jnp.broadcast_to(eig_y[...], (8, block))), split(to_q))
    ecol = jnp.sum(is_p * eig_x[...], axis=1, keepdims=True)
    ecol = jnp.where(iota((npad, 1), 0) < pairs, ecol, 1.0)
    inverse = 1.0 / (ecol + eig_yz[0:1])
    own = dot3(split(w_out * w_out), split(inverse))
    w_out = split(w_out)

    wait_all(halo)
    cx[...] = c_main + dot3(split(rim[...].T), k_rim)

    right = {"ex": wrap(ix + 1, nx)}
    left = {"ex": wrap(ix - 1, nx)}

    def x_copies():
        return (
            shipped(cx.at[pl.ds(length - 1, 1)], hx.at[pl.ds(0, 1)], 16, right),
            shipped(cx.at[pl.ds(0, 1)], hx.at[pl.ds(8, 1)], 17, left),
        )

    def v_copies():
        return (
            shipped(vs.at[pl.ds(8, 1)], vr.at[pl.ds(0, 1)], 18, right),
            shipped(vs.at[pl.ds(0, 1)], vr.at[pl.ds(8, 1)], 19, left),
        )

    for c in x_copies():
        c.start()
    modal = dot3(w_main, split(cx[...]))
    vs[...] = dot3(w_out, split(modal * inverse))
    for c in v_copies():
        c.start()
    mine[1, :, :nm] = stage_end("ez")
    stage_start("ex")
    for c in x_copies():
        c.wait()
    modal = modal + dot3(w_halo, split(hx[...]))
    us[...] = dot3(w_back, split(modal * inverse))
    for c in v_copies():
        c.wait()
    us[0:1] += vr[0:1] + own[8:9] * cx[0:1]
    us[length - 1 : length] += vr[8:9] + own[0:1] * cx[length - 1 : length]
    u = split(us[...])
    back[...] = dot3(k_rim, u, (1, 1))
    start_all(ret)
    mine[2, :, :nm] = stage_end("ex")
    stage_start("ey")
    result = dot3(k_main, u, (1, 1))
    scaled = split(stage_end("ey") / level)
    coarse = dot3(split(amat.T), scaled)
    coarse = dot3(split(coarse), wxm, (1, 1))
    result = result + dot3(hyz, split(coarse), (0, 0))
    out[...] = result.reshape(n, n, length)
    wait_all(ret)
    out[n - 1] += got[0:n]
    out[0] += got[n : 2 * n]
    out[:, n - 1] += got[2 * n : 3 * n]
    out[:, 0] += got[3 * n : 4 * n]
    for e in range(4):
        k, j = (n - 1, 0)[e >> 1], (n - 1, 0)[e & 1]
        out[k, j : j + 1] += got[4 * n + e : 4 * n + e + 1]


def per_device(sizes, residual, local_stream, local_normal, local_span, eigen_stream, eigen_normal,
               eigen_span, vertex_stream, vertex_normal, vertex_span, level_stream, level_normal,
               level_span):
    nx, ny, nz = sizes
    block = local_stream.shape[0]
    n = block - 2
    length = residual.shape[2]
    rows = n * n + 4 * n + 16
    lanes = -(-block * block // 128) * 128
    mn = ny * nz
    copies = 20 + nx + ny + nz - 3
    vmem = pl.BlockSpec(memory_space=pltpu.VMEM)
    args = (
        residual, local_stream, local_normal.transpose(1, 0, 2), local_span,
        eigen_stream.reshape(1, -1), eigen_normal, eigen_span.reshape(1, -1), vertex_stream,
        vertex_normal, vertex_span, level_stream.reshape(1, -1), level_normal.reshape(1, -1),
        level_span.reshape(1, -1),
    )
    return pl.pallas_call(
        functools.partial(kernel, sizes),
        out_shape=pltpu.VMEM(residual.shape, F32),
        in_specs=[pl.BlockSpec(memory_space=pltpu.HBM)] * 13,
        out_specs=vmem,
        scratch_shapes=[
            pltpu.VMEM((rows - n * n, length), F32),
            pltpu.VMEM((rows, lanes), BF16),
            pltpu.VMEM((rows, lanes), BF16),
            pltpu.VMEM((length, lanes), F32),
            pltpu.VMEM((rows - n * n, length), F32),
            pltpu.VMEM((rows - n * n, length), F32),
            pltpu.VMEM((nx + ny + nz - 3, mn, 128), F32),
            pltpu.VMEM((3, mn, 128), F32),
            pltpu.VMEM((16, lanes), F32),
            pltpu.VMEM((16, lanes), F32),
            pltpu.VMEM((16, lanes), F32),
            pltpu.VMEM((length, lanes), F32),
            pltpu.SemaphoreType.DMA((copies,)),
            pltpu.SemaphoreType.DMA((copies,)),
            pltpu.SemaphoreType.DMA((13,)),
        ] + [pltpu.VMEM(a.shape, F32) for a in args],
        compiler_params=pltpu.CompilerParams(
            collective_id=0, has_side_effects=True
        ),
    )(*args)


def solution(mesh):
    sizes = (mesh.shape["ex"], mesh.shape["ey"], mesh.shape["ez"])
    placed = (P("ez", "ey", "ex"), P(), P("ey", None, None), P(), P(), P("ey", None)) + (P(),) * 7
    return jax.shard_map(
        functools.partial(per_device, sizes), mesh=mesh, in_specs=placed,
        out_specs=P("ez", "ey", "ex"), check_vma=False,
    )
```

```python
import functools
import math

import jax
import jax.numpy as jnp
from jax import lax
from jax.experimental import pallas as pl
from jax.experimental.pallas import tpu as pltpu
from jax.sharding import PartitionSpec as P

F32 = jnp.float32
BF16 = jnp.bfloat16
I32 = jnp.int32
DIRS = ((1, 0), (-1, 0), (0, 1), (0, -1), (1, 1), (1, -1), (-1, 1), (-1, -1))


def iota(shape, dim):
    return lax.broadcasted_iota(I32, shape, dim)


def quotient(x, d):
    return (x * (65536 // d + 1)) >> 16


def onehot(mask):
    return jnp.where(mask, 1.0, 0.0).astype(F32)


def split(x):
    hi = x.astype(BF16)
    return hi, (x - hi.astype(F32)).astype(BF16)


def dg(a, b, dims):
    return lax.dot_general(a, b, ((dims[:1], dims[1:]), ((), ())), preferred_element_type=F32)


def dot3(a, b, dims=(1, 0)):
    (ah, al), (bh, bl) = a, b
    return dg(ah, bh, dims) + (dg(ah, bl, dims) + dg(al, bh, dims))


def pick(mask, values, dims=(1, 0)):
    hi, lo = split(values)
    mask = mask.astype(BF16)
    return dg(mask, hi, dims) + dg(mask, lo, dims)


def hat(index, points):
    out = jnp.zeros(index.shape, F32)
    for i in range(points):
        out = jnp.where(index == i, (1.0 - math.cos(math.pi * i / (points - 1))) / 2.0, out)
    return out


def kernel(
    sizes,
    *refs,
):
    inputs, out = refs[:13], refs[13]
    rim, kh, kl, cx, back, got, parts, mine, hx, vs, vr, us, ssem, rsem, isem = refs[14:29]
    held = refs[29:]
    (
        res, stream, normal, span, eig_x, eig_y, eig_z,
        v_stream, v_normal, v_span, lev_x, lev_y, lev_z,
    ) = held
    for i in range(13):
        pltpu.make_async_copy(inputs[i], held[i], isem.at[i]).start()
    nx, ny, nz = sizes
    block = stream.shape[0]
    n = block - 2
    sh = n.bit_length() - 1
    length = res.shape[2]
    ne = length // n
    main = n * n
    rows = kh.shape[0]
    nrim = rows - main
    lanes = kh.shape[1]
    edge = main + 4 * n
    nv, nm = v_stream.shape
    mn = nz * ny
    ix, iy, iz = lax.axis_index("ex"), lax.axis_index("ey"), lax.axis_index("ez")

    rim[...] = jnp.zeros_like(rim)
    got[...] = jnp.zeros_like(got)
    hx[...] = jnp.zeros_like(hx)

    def wrap(i, size):
        return lax.rem(i + size, size)

    def has(dy):
        return jnp.logical_and(iy + dy >= 0, iy + dy < ny)

    def guarded(dy, fn):
        if dy == 0:
            fn()
        else:
            pl.when(has(dy))(fn)

    barrier = pltpu.get_barrier_semaphore()

    def signal(where):
        pl.semaphore_signal(
            barrier, inc=1, device_id=where, device_id_type=pl.DeviceIdType.MESH
        )

    for axis, index, size in (("ez", iz, nz), ("ey", iy, ny), ("ex", ix, nx)):
        for d in range(1, size):
            signal({axis: lax.rem(index + d, size)})
    for dz, dy in DIRS[4:]:
        guarded(dy, functools.partial(signal, {"ez": wrap(iz + dz, nz), "ey": iy + dy}))
    inner = jnp.where(iy > 0, 2, 0) + jnp.where(iy < ny - 1, 2, 0)

    pltpu.make_async_copy(inputs[0], held[0], isem.at[0]).wait()
    pl.semaphore_wait(barrier, (nx - 1) + (ny - 1) + (nz - 1) + inner)

    def shipped(src, dst, slot, where):
        return pltpu.make_async_remote_copy(
            src_ref=src, dst_ref=dst, send_sem=ssem.at[slot], recv_sem=rsem.at[slot],
            device_id=where, device_id_type=pl.DeviceIdType.MESH,
        )

    def target(dz, dy):
        where = {}
        if dz:
            where["ez"] = wrap(iz + dz, nz)
        if dy:
            where["ey"] = iy + dy
        return where

    def halo(slot):
        dz, dy = DIRS[slot]
        if dy == 0:
            src = res.at[n - 1 if dz > 0 else 0]
            dst = rim.at[pl.ds(0 if dz > 0 else n, n)]
        elif dz == 0:
            src = res.at[:, n - 1 if dy > 0 else 0]
            dst = rim.at[pl.ds(2 * n if dy > 0 else 3 * n, n)]
        else:
            src = res.at[n - 1 if dz > 0 else 0, pl.ds(n - 1 if dy > 0 else 0, 1)]
            dst = rim.at[pl.ds(4 * n + (0 if dz > 0 else 2) + (0 if dy > 0 else 1), 1)]
        return shipped(src, dst, slot, target(dz, dy))

    def ret(slot):
        dz, dy = DIRS[slot]
        if dy == 0:
            at, number = (n if dz > 0 else 0), n
        elif dz == 0:
            at, number = (3 * n if dy > 0 else 2 * n), n
        else:
            at, number = 4 * n + (2 if dz > 0 else 0) + (1 if dy > 0 else 0), 1
        return shipped(
            back.at[pl.ds(at, number)], got.at[pl.ds(at, number)], 8 + slot, target(dz, dy)
        )

    def start_all(make):
        for s, (dz, dy) in enumerate(DIRS):
            guarded(dy, lambda s=s: make(s).start())

    def wait_all(make):
        for s, (dz, dy) in enumerate(DIRS):
            guarded(dy, lambda s=s: make(s).wait_send())
            guarded(-dy, lambda s=s: make(s).wait_recv())

    stages = {"ex": (0, ix, nx), "ez": (1, iz, nz), "ey": (2, iy, ny)}
    offset = {"ez": 0, "ex": nz - 1, "ey": nz + nx - 2}

    def stage_copies(axis):
        st, index, size = stages[axis]
        return [
            shipped(
                mine.at[st], parts.at[offset[axis] + d - 1], 20 + offset[axis] + d - 1,
                {axis: lax.rem(index + d, size)},
            )
            for d in range(1, size)
        ]

    def stage_start(axis):
        for c in stage_copies(axis):
            c.start()

    def stage_end(axis):
        st, index, size = stages[axis]
        total = mine[st, :, :nm]
        for d, c in enumerate(stage_copies(axis)):
            c.wait_recv()
            c.wait_send()
            total = total + parts[offset[axis] + d, :, :nm]
        return total

    start_all(halo)
    for i in range(1, 13):
        pltpu.make_async_copy(inputs[i], held[i], isem.at[i]).wait()
    data = res[...].reshape(main, length)
    row, col = iota((rows, block), 0), iota((rows, block), 1)
    low = row & (n - 1)
    e0 = row - edge
    rk = jnp.where(row < main, (row >> sh) + 1, low + 1)
    rk = jnp.where((row >= main) & (row < main + n), 0, rk)
    rk = jnp.where((row >= main + n) & (row < main + 2 * n), n + 1, rk)
    rk = jnp.where(row >= edge, jnp.where(e0 < 2, 0, n + 1), rk)
    rk = jnp.where(row >= edge + 4, -1, rk)
    rj = jnp.where((row >= main + 2 * n) & (row < main + 3 * n), 0, low + 1)
    rj = jnp.where((row >= main + 3 * n) & (row < main + 4 * n), n + 1, rj)
    rj = jnp.where(row >= edge, jnp.where((e0 & 1) == 0, 0, n + 1), rj)
    rj = jnp.where(row >= edge + 4, -1, rj)
    sel_k, sel_j = onehot(rk == col), onehot(rj == col)
    brow, bcol = iota((block, lanes), 0), iota((block, lanes), 1)
    bq = quotient(bcol, block)
    to_r = onehot(bq == brow)
    to_q = onehot((bcol - block * bq == brow) & (bcol < block * block))
    span_l = dot3(split(span[...]), split(to_r))
    normal_l = dot3(split(normal[...].reshape(block, block)), split(to_q))
    kmat = pick(sel_k, span_l) * pick(sel_j, normal_l)
    k_hi, k_lo = split(kmat)
    kh[...] = k_hi
    kl[...] = k_lo

    wn = n
    hrow, hcol = iota((8, main), 0), iota((8, main), 1)
    wk, wj = hat(hcol >> sh, wn), hat(hcol & (n - 1), wn)
    hyz = jnp.where((hrow & 2) > 0, wk, 1.0 - wk) * jnp.where((hrow & 1) > 0, wj, 1.0 - wj)
    hyz = split(jnp.where(hrow < 4, hyz, 0.0))
    xrow, xcol = iota((length, nv), 0), iota((length, nv), 1)
    wx = hat(xrow & (n - 1), wn)
    base = ix * ne + (xrow >> sh)
    after = jnp.where(base + 1 >= nv, base + 1 - nv, base + 1)
    hatx = jnp.where(xcol == base, 1.0 - wx, 0.0) + jnp.where(xcol == after, wx, 0.0)
    wxm = split(dot3(split(hatx), split(v_stream[...])))
    d_split = split(data)
    loads = dot3(split(dot3(hyz, d_split)), wxm)
    mrow, mcol = iota((mn, nz), 0), iota((mn, nz), 1)
    is_m = onehot((mrow >= mcol * ny) & (mrow < (mcol + 1) * ny))
    nrow, ncol = iota((mn, ny), 0), iota((mn, ny), 1)
    is_n = onehot(nrow - ny * quotient(nrow, ny) == ncol)
    vrow, vcol = iota((nz, 8), 0), iota((nz, 8), 1)
    vz = iz + (vcol >> 1)
    vz = jnp.where(vz >= nz, vz - nz, vz)
    at_z = onehot((vrow == vz) & (vcol < 4))
    urow, ucol = iota((ny, 8), 0), iota((ny, 8), 1)
    at_y = onehot((urow == iy + (ucol & 1)) & (ucol < 4))
    amat = pick(is_m, dot3(split(v_span[...].T), split(at_z)))
    amat = amat * pick(is_n, dot3(split(v_normal[...].T), split(at_y)))
    a_split = split(amat)
    mine[0, :, :nm] = dot3(a_split, split(loads))
    level = jnp.sum(is_m * lev_z[...], axis=1, keepdims=True)
    level = level + jnp.sum(is_n * lev_y[...], axis=1, keepdims=True) + lev_x[...]

    stage_start("ex")
    k_main = kh[0:main], kl[0:main]
    k_rim = kh[main:], kl[main:]
    c_main = dot3(split(data.T), k_main)
    nep = length + 16
    pairs = ne * block
    npad = -(-pairs // 16) * 16

    def place(c):
        far = jnp.where(c == length + 8, length, -n * length)
        return jnp.where(c < length, c, jnp.where(c == length, -1, far))

    wrow, wcol = iota((npad, nep), 0), iota((npad, nep), 1)
    xi = place(wcol) + 1 - n * quotient(wrow, block)
    trow, tcol = iota((block, nep), 0), iota((block, nep), 1)
    tx = place(tcol)
    tm = (tx + 1) & (n - 1)
    s_t = split(stream[...].T)
    first = dot3(s_t, split(onehot(trow == tm)))
    second = dot3(s_t, split(onehot(trow - n == tm)))
    prow, pcol = iota((npad, block), 0), iota((npad, block), 1)
    is_p = onehot((prow - block * quotient(prow, block) == pcol) & (prow < pairs))
    wmat = jnp.where((xi >= 0) & (xi < n), pick(is_p, first), 0.0)
    wmat = wmat + jnp.where((xi >= n) & (xi < block), pick(is_p, second), 0.0)
    w_main = split(wmat[:, :length])
    w_halo = split(wmat[:, length:])
    w_out = wmat[:, length:].T
    w_back = split(wmat[:, :length].T)
    eig_yz = dot3(split(jnp.broadcast_to(eig_z[...], (8, block))), split(to_r))
    eig_yz = eig_yz + dot3(split(jnp.broadcast_to(eig_y[...], (8, block))), split(to_q))
    ecol = jnp.sum(is_p * eig_x[...], axis=1, keepdims=True)
    ecol = jnp.where(iota((npad, 1), 0) < pairs, ecol, 1.0)
    inverse = 1.0 / (ecol + eig_yz[0:1])
    own = dot3(split(w_out * w_out), split(inverse))
    w_out = split(w_out)

    wait_all(halo)
    cx[...] = c_main + dot3(split(rim[...].T), k_rim)

    right = {"ex": wrap(ix + 1, nx)}
    left = {"ex": wrap(ix - 1, nx)}

    def x_copies():
        return (
            shipped(cx.at[pl.ds(length - 1, 1)], hx.at[pl.ds(0, 1)], 16, right),
            shipped(cx.at[pl.ds(0, 1)], hx.at[pl.ds(8, 1)], 17, left),
        )

    def v_copies():
        return (
            shipped(vs.at[pl.ds(8, 1)], vr.at[pl.ds(0, 1)], 18, right),
            shipped(vs.at[pl.ds(0, 1)], vr.at[pl.ds(8, 1)], 19, left),
        )

    for c in x_copies():
        c.start()
    modal = dot3(w_main, split(cx[...]))
    vs[...] = dot3(w_out, split(modal * inverse))
    for c in v_copies():
        c.start()
    mine[1, :, :nm] = stage_end("ex")
    stage_start("ez")
    mine[2, :, :nm] = stage_end("ez")
    stage_start("ey")
    for c in x_copies():
        c.wait()
    modal = modal + dot3(w_halo, split(hx[...]))
    us[...] = dot3(w_back, split(modal * inverse))
    for c in v_copies():
        c.wait()
    us[0:1] += vr[0:1] + own[8:9] * cx[0:1]
    us[length - 1 : length] += vr[8:9] + own[0:1] * cx[length - 1 : length]
    u = split(us[...])
    back[...] = dot3(k_rim, u, (1, 1))
    start_all(ret)
    result = dot3(k_main, u, (1, 1))
    scaled = split(stage_end("ey") / level)
    coarse = dot3(split(amat.T), scaled)
    coarse = dot3(split(coarse), wxm, (1, 1))
    result = result + dot3(hyz, split(coarse), (0, 0))
    out[...] = result.reshape(n, n, length)
    wait_all(ret)
    out[n - 1] += got[0:n]
    out[0] += got[n : 2 * n]
    out[:, n - 1] += got[2 * n : 3 * n]
    out[:, 0] += got[3 * n : 4 * n]
    for e in range(4):
        k, j = (n - 1, 0)[e >> 1], (n - 1, 0)[e & 1]
        out[k, j : j + 1] += got[4 * n + e : 4 * n + e + 1]


def per_device(sizes, residual, local_stream, local_normal, local_span, eigen_stream, eigen_normal,
               eigen_span, vertex_stream, vertex_normal, vertex_span, level_stream, level_normal,
               level_span):
    nx, ny, nz = sizes
    block = local_stream.shape[0]
    n = block - 2
    length = residual.shape[2]
    rows = n * n + 4 * n + 16
    lanes = -(-block * block // 128) * 128
    mn = ny * nz
    copies = 20 + nx + ny + nz - 3
    vmem = pl.BlockSpec(memory_space=pltpu.VMEM)
    args = (
        residual, local_stream, local_normal.transpose(1, 0, 2), local_span,
        eigen_stream.reshape(1, -1), eigen_normal, eigen_span.reshape(1, -1), vertex_stream,
        vertex_normal, vertex_span, level_stream.reshape(1, -1), level_normal.reshape(1, -1),
        level_span.reshape(1, -1),
    )
    return pl.pallas_call(
        functools.partial(kernel, sizes),
        out_shape=pltpu.VMEM(residual.shape, F32),
        in_specs=[pl.BlockSpec(memory_space=pltpu.HBM)] * 13,
        out_specs=vmem,
        scratch_shapes=[
            pltpu.VMEM((rows - n * n, length), F32),
            pltpu.VMEM((rows, lanes), BF16),
            pltpu.VMEM((rows, lanes), BF16),
            pltpu.VMEM((length, lanes), F32),
            pltpu.VMEM((rows - n * n, length), F32),
            pltpu.VMEM((rows - n * n, length), F32),
            pltpu.VMEM((nx + ny + nz - 3, mn, 128), F32),
            pltpu.VMEM((3, mn, 128), F32),
            pltpu.VMEM((16, lanes), F32),
            pltpu.VMEM((16, lanes), F32),
            pltpu.VMEM((16, lanes), F32),
            pltpu.VMEM((length, lanes), F32),
            pltpu.SemaphoreType.DMA((copies,)),
            pltpu.SemaphoreType.DMA((copies,)),
            pltpu.SemaphoreType.DMA((13,)),
        ] + [pltpu.VMEM(a.shape, F32) for a in args],
        compiler_params=pltpu.CompilerParams(
            collective_id=0, has_side_effects=True
        ),
    )(*args)


def solution(mesh):
    sizes = (mesh.shape["ex"], mesh.shape["ey"], mesh.shape["ez"])
    placed = (P("ez", "ey", "ex"), P(), P("ey", None, None), P(), P(), P("ey", None)) + (P(),) * 7
    return jax.shard_map(
        functools.partial(per_device, sizes), mesh=mesh, in_specs=placed,
        out_specs=P("ez", "ey", "ex"), check_vma=False,
    )
```
